512 devices in a mesh: seq: 32 (over z, core), tp: 16 (over y, x).
Axes of the slice: x: 4, y: 4, z: 16, core: 2. Of those that a mesh axis runs over, the one named last changes fastest.
Arguments:
- tokens: bfloat16 [8192, 4096], P('seq', 'tp'), may hold values from -400 to 400
- light_qkv: bfloat16 [4096, 32, 384], P('seq', 'tp'), may hold values from -40 to 40
- heavy_qkv: bfloat16 [4096, 32, 384], P('seq', 'tp'), may hold values from -40 to 40
- ffn_in: bfloat16 [4096, 2048], P('seq', 'tp'), may hold values from -0.09375 to 0.09375
- light_out: bfloat16 [4096, 32, 128], P('seq', 'tp'), may hold values from -1 to 1
- heavy_out: bfloat16 [4096, 32, 128], P('seq', 'tp'), may hold values from -1 to 1
- ffn_out: bfloat16 [4096, 2048], P('seq', 'tp'), may hold values from -0.25 to 0.25
- picks: int32 [64, 16], P('seq'), may hold values from -1 to 127, as said below
Outputs:
- mixed: bfloat16 [8192, 4096], P('seq', 'tp')
The draws below stay inside these ranges and needn't reach their ends.
Inputs may be any that keep to these rules, and one draw needn't show every extreme that they name: `picks`: row b lists distinct positions within block b in rising order, then -1 in the remaining slots. Every run of 256 tokens starting at a multiple of 256 holds at least one block with 16 picked positions.
All inputs are finite; a program needn't handle non-finite values.
Results may differ from the reference program's by a relative error of at most 0.015.
Values may be sent and summed in bfloat16 or wider, within the bound.
A program may use at most 64 MiB of HBM per device.

```python
import math
import jax
import jax.numpy as jnp
from jax import lax

D = 4096
HD = 128
BLOCK = 128
TOK_DEV = 256
HEADS = 32
FF = 2048
CAP = 16
TOKENS = 8192
NBLK = 64
SLOTS = 1024
N_TP = 16


def draw_tokens(key, part):
    row_key, column_key, base_key = jax.random.split(key, 3)
    row_scale = jnp.exp(jax.random.uniform(row_key, (TOKENS, 1), jnp.float32, 0.0, math.log(10.0)))
    column_scale = jnp.exp(jax.random.uniform(column_key, (1, D), jnp.float32, 0.0, math.log(10.0)))
    base_draw = jax.random.truncated_normal(base_key, -4.0, 4.0, (TOKENS, D), jnp.float32)
    return (base_draw * row_scale * column_scale).astype(jnp.bfloat16)


def attention_weights(key):
    query_key, key_key, value_key = jax.random.split(key, 3)
    fan_scale = D ** (-0.5)
    weight_shape = (D, HEADS, HD)
    query_part = jax.random.truncated_normal(query_key, -6.0, 6.0, weight_shape, jnp.float32) * (2.0 * fan_scale)
    key_part = jax.random.truncated_normal(key_key, -6.0, 6.0, weight_shape, jnp.float32) * fan_scale
    value_part = jax.random.truncated_normal(value_key, -6.0, 6.0, weight_shape, jnp.float32) * fan_scale
    return jnp.concatenate([query_part, key_part, value_part], axis=2).astype(jnp.bfloat16)


def draw_light_qkv(key, part):
    return attention_weights(jax.random.fold_in(key, 11))


def draw_heavy_qkv(key, part):
    return attention_weights(jax.random.fold_in(key, 23))


def draw_picks(key, part):
    floor_key, count_key, full_key, order_key = jax.random.split(jax.random.fold_in(key, 37), 4)
    shards = TOKENS // TOK_DEV
    per_shard = TOK_DEV // BLOCK
    shard_floor = jax.random.randint(floor_key, (shards, 1), 0, CAP + 1, dtype=jnp.int32)
    counts = jnp.maximum(jax.random.randint(count_key, (shards, per_shard), 0, CAP + 1, dtype=jnp.int32), shard_floor)
    full_at = jax.random.randint(full_key, (shards, 1), 0, per_shard, dtype=jnp.int32)
    counts = jnp.where(jnp.arange(per_shard, dtype=jnp.int32)[None, :] == full_at, CAP, counts).reshape(NBLK)
    scores = jax.random.randint(order_key, (NBLK, BLOCK), 0, 2 ** 20, dtype=jnp.int32) * BLOCK + jnp.arange(BLOCK, dtype=jnp.int32)[None, :]
    ranking = jnp.argsort(scores, axis=1)[:, :CAP].astype(jnp.int32)
    chosen = jnp.sort(ranking, axis=1)
    return jnp.where(jnp.arange(CAP, dtype=jnp.int32)[None, :] < counts[:, None], chosen, -1).astype(jnp.int32)


def with_spikes(entries, rng, source, target, blocks, factor):
    owner, partner = [(jnp.arange(entries.shape[dim]) // (entries.shape[dim] // blocks)).reshape([-1 if axis == dim else 1 for axis in range(entries.ndim)]) for dim in (source, target)]
    chosen = jax.random.permutation(rng, blocks)[partner]
    strong = (owner == chosen) | (owner == (partner + blocks // 2) % blocks)
    return jnp.where(strong, factor * entries, entries)


def shard_levels(key, extent, pieces, least, top_value):
    gain, own = 1.0, jax.random.fold_in(key, 6)
    for dim, parts in pieces:
        heights = jnp.exp(jax.random.uniform(jax.random.fold_in(own, dim), (parts,), jnp.float32, least / len(pieces), top_value / len(pieces)))
        gain = gain * jnp.repeat(heights, extent[dim] // parts).reshape([-1 if axis == dim else 1 for axis in range(len(extent))])
    return gain


def bell_draw(key, dims, deviation, limit, cuts=(), kind=jnp.bfloat16):
    factor_of = shard_levels(key, dims, cuts, -0.22, 0.18) if cuts else 1.0
    drawn = jax.random.normal(key, dims, jnp.float32) * deviation * factor_of
    return jnp.minimum(jnp.maximum(drawn, -limit), limit).astype(kind)


def heavy_noise(key, extent, scale, most, cuts, heavy, held_as=jnp.bfloat16):
    array = scale * jax.random.normal(key, extent, jnp.float32)
    if cuts:
        array = array * shard_levels(key, extent, cuts, -0.22, 0.18)
    return jnp.clip(with_spikes(array, jax.random.fold_in(key, 3), *heavy), -most, most).astype(held_as)


def setup_inputs(seed: int = 0) -> dict:
    splits = jax.random.split(jax.random.key(seed), 9)
    tokens = draw_tokens(jax.random.fold_in(splits[8], 71), 0)
    light_qkv = draw_light_qkv(jax.random.fold_in(splits[8], 71), 0)
    heavy_qkv = draw_heavy_qkv(jax.random.fold_in(splits[8], 71), 0)
    ffn_in = bell_draw(splits[3], (D, FF), D ** -0.5, 0.09375, ((0, 32), (1, 16)))
    light_out = heavy_noise(splits[4], (D, HEADS, HD), HD ** -0.5, 1.0, ((0, 32), (1, 16)), (1, 0, 32, 2.75))
    heavy_out = heavy_noise(splits[5], (D, HEADS, HD), HD ** -0.5, 1.0, ((0, 32), (1, 16)), (1, 0, 32, 2.75))
    ffn_out = heavy_noise(splits[6], (D, FF), FF ** -0.5, 0.25, ((0, 32), (1, 16)), (1, 0, 32, 2.75))
    picks = draw_picks(jax.random.fold_in(splits[8], 71), 0)
    return dict(tokens=tokens, light_qkv=light_qkv, heavy_qkv=heavy_qkv, ffn_in=ffn_in, light_out=light_out, heavy_out=heavy_out, ffn_out=ffn_out, picks=picks)


NEGATIVE = -1e+30

def normalize(row_values):
    values = row_values.astype(jnp.float32)
    factor = lax.rsqrt(lax.optimization_barrier(jnp.mean(values * values, axis=-1, keepdims=True)) + 1e-06)
    return (values * factor).astype(jnp.bfloat16)

def softmax_apply(scores, allowed, value_part):
    scores = jnp.where(allowed, scores, NEGATIVE)
    row_top = lax.optimization_barrier(jnp.max(scores, axis=-1, keepdims=True))
    weights_raw = jnp.where(allowed, jnp.exp(scores - row_top), 0.0)
    rounded = lax.optimization_barrier(weights_raw.astype(jnp.bfloat16)).astype(jnp.float32)
    output = jnp.einsum('...qk,...kd->...qd', rounded, value_part.astype(jnp.float32))
    return output / lax.optimization_barrier(jnp.sum(weights_raw, axis=-1, keepdims=True))

def local_head(query_part, key_values, score_scale):
    blocks = TOKENS // BLOCK
    head_size = query_part.shape[1]
    padded = jnp.pad(key_values, ((BLOCK, BLOCK), (0, 0)))
    grouped = padded.reshape(blocks + 2, BLOCK, 2 * head_size)
    window = jnp.concatenate([grouped[:-2], grouped[1:-1], grouped[2:]], axis=1)
    query_blocks = query_part.reshape(blocks, BLOCK, head_size).astype(jnp.float32)
    scores = jnp.einsum('gqd,gkd->gqk', query_blocks, window[..., :head_size].astype(jnp.float32)) * score_scale
    position = (jnp.arange(blocks, dtype=jnp.int32)[:, None] - 1) * BLOCK + jnp.arange(3 * BLOCK, dtype=jnp.int32)[None, :]
    inside = ((position >= 0) & (position < TOKENS))[:, None, :]
    output = softmax_apply(scores, inside, window[..., head_size:])
    return output.astype(jnp.bfloat16).reshape(TOKENS, head_size)

def global_head(query_part, key_values, slot_live, score_scale):
    head_size = query_part.shape[1]
    scores = jnp.einsum('qd,kd->qk', query_part.astype(jnp.float32), key_values[:, :head_size].astype(jnp.float32)) * score_scale
    output = softmax_apply(scores, slot_live[None, :], key_values[:, head_size:])
    return output.astype(jnp.bfloat16)

def reference(tokens, light_qkv, heavy_qkv, ffn_in, light_out, heavy_out, ffn_out, picks):
    head_count = light_qkv.shape[1]
    head_size = light_qkv.shape[2] // 3
    score_scale = head_size ** (-0.5)
    normed = normalize(tokens)
    light_all = jnp.dot(normed, light_qkv.reshape(D, -1), preferred_element_type=jnp.float32)
    light_all = light_all.astype(jnp.bfloat16).reshape(TOKENS, head_count, 3 * head_size)
    light_heads = lax.map(lambda operands: local_head(operands[0], operands[1], score_scale), (jnp.moveaxis(light_all[:, :, :head_size], 1, 0), jnp.moveaxis(light_all[:, :, head_size:], 1, 0)))
    light_heads = jnp.moveaxis(light_heads, 0, 1)
    slot_live = (picks >= 0).reshape(-1)
    token_index = (jnp.arange(NBLK, dtype=jnp.int32)[:, None] * BLOCK + jnp.maximum(picks, 0)).reshape(-1).astype(jnp.int32)
    picked = normed[token_index]
    heavy_all = jnp.dot(picked, heavy_qkv.reshape(D, -1), preferred_element_type=jnp.float32)
    heavy_all = heavy_all.astype(jnp.bfloat16).reshape(SLOTS, head_count, 3 * head_size)
    heavy_heads = lax.map(lambda operands: global_head(operands[0], operands[1], slot_live, score_scale), (jnp.moveaxis(heavy_all[:, :, :head_size], 1, 0), jnp.moveaxis(heavy_all[:, :, head_size:], 1, 0)))
    heavy_heads = jnp.moveaxis(heavy_heads, 0, 1).astype(jnp.float32) * slot_live[:, None, None].astype(jnp.float32)
    heavy_rows = jnp.zeros((TOKENS, head_count, head_size), jnp.float32).at[token_index].add(heavy_heads)
    heavy_rows = heavy_rows.astype(jnp.bfloat16)
    ffn_hidden = jax.nn.gelu(jnp.dot(normed, ffn_in, preferred_element_type=jnp.float32)).astype(jnp.bfloat16)
    heads_local = head_count // N_TP
    hidden_local = ffn_in.shape[1] // N_TP
    activations = jnp.concatenate([light_heads.reshape(TOKENS, N_TP, heads_local * head_size), heavy_rows.reshape(TOKENS, N_TP, heads_local * head_size), ffn_hidden.reshape(TOKENS, N_TP, hidden_local)], axis=2)
    weights = jnp.concatenate([light_out.reshape(D, N_TP, heads_local * head_size), heavy_out.reshape(D, N_TP, heads_local * head_size), ffn_out.reshape(D, N_TP, hidden_local)], axis=2)

    def add_group(running, operands):
        group_acts, group_weights = operands
        partial_value = lax.dot_general(group_acts, group_weights, (((1,), (1,)), ((), ())), preferred_element_type=jnp.float32)
        partial_value = lax.optimization_barrier(partial_value.astype(jnp.bfloat16)).astype(jnp.float32)
        return (running + partial_value, None)
    running, _ = lax.scan(add_group, jnp.zeros((TOKENS, D), jnp.float32), (jnp.moveaxis(activations, 1, 0), jnp.moveaxis(weights, 1, 0)))
    return running.astype(jnp.bfloat16)
```

```python
import functools
import types

import jax
import jax.numpy as jnp
from jax import lax
from jax.experimental import pallas as pl
from jax.experimental.pallas import tpu as pltpu
from jax.sharding import PartitionSpec as P

MESH = pl.DeviceIdType.MESH
NEGATIVE = -1e30
BF = jnp.bfloat16
F32 = jnp.float32


def nt(left, right):
    return lax.dot_general(left, right, (((1,), (1,)), ((), ())), preferred_element_type=F32)


def nn(left, right):
    return jnp.dot(left, right, preferred_element_type=F32)


def gelu(v):
    return 0.5 * v * (1.0 + jnp.tanh(0.7978845608028654 * (v + 0.044715 * (v * v * v))))


def kernel(
    cfg,
    tok_ref,
    lq_ref,
    fi_ref,
    lo_ref,
    fo_ref,
    hq_ref,
    ho_ref,
    sel_ref,
    selt_ref,
    kmask_ref,
    out_ref,
    x,
    w1,
    w2,
    w3,
    w4,
    kvg,
    acc,
    qb,
    kvb,
    halo,
    act,
    picked,
    hacc,
    hq,
    rs_send,
    rs_recv,
    hs_send,
    hs_recv,
    osum,
    zs,
    zr,
    ps,
    pr,
    ls,
    ts,
    tr,
    rss,
    rsr,
    hss,
    hsr,
    hls,
    hlr,
):
    Z, T, SX, SY = cfg.z, cfg.tp, cfg.sx, cfg.sy
    NA, NB = Z // 2, Z // 2 - 1
    S = 2 * Z
    seq = lax.axis_index("seq")
    t = lax.axis_index("tp")
    z = seq // 2
    c = seq % 2
    sg = 1 - 2 * c
    tx, ty = t % SX, t // SX
    scale = 128.0 ** -0.5

    def zmod(v):
        return (v + 2 * Z) % Z

    def rel(k):
        return ((ty + k // SX) % SY) * SX + (tx + k % SX) % SX

    partner = (z * 2 + 1 - c, t)
    nxt = ((zmod(z + sg) * 2 + c, t), (zmod(z - sg) * 2 + c, t))
    left = ((seq + S - 1) % S, t)
    right = ((seq + 1) % S, t)

    def phase(i, buf, rows, pieces, flat=False):
        return types.SimpleNamespace(i=i, buf=buf, rows=rows, nh=pieces, flat=flat)

    p1 = phase(0, w1, 128, 2)
    p2 = phase(1, w2, 128, 2)
    p3 = phase(2, w3, 128, 2)
    p4 = phase(3, w4, 128, 2)
    pk = phase(4, kvg, 32, 1, True)

    def piece(ph, zz, cc, h):
        n = ph.rows // ph.nh
        if ph.flat:
            return ph.buf.at[pl.ds(pl.multiple_of((zz * 2 + cc) * ph.rows + h * n, n), n)]
        return ph.buf.at[zz, pl.ds(pl.multiple_of(cc * ph.rows + h * n, n), n)]

    def source(dr, d):
        return zmod(z - sg * d) if dr == 0 else zmod(z + sg * d)

    def zcopy(ph, dr, d, h):
        ref = piece(ph, source(dr, d - 1), c, h)
        return pltpu.make_async_remote_copy(
            ref, ref, zs.at[ph.i, dr, h, d], zr.at[ph.i, dr, h, d], nxt[dr], MESH
        )

    def zarrive(ph, dr, d, h):
        ref = piece(ph, source(dr, d), c, h)
        return pltpu.make_async_remote_copy(
            ref, ref, zs.at[ph.i, dr, h, d], zr.at[ph.i, dr, h, d], nxt[1 - dr], MESH
        )

    def pcopy(ph, dr, d, h):
        ref = piece(ph, source(dr, d), c, h)
        return pltpu.make_async_remote_copy(
            ref, ref, ps.at[ph.i, dr, h, d], pr.at[ph.i, dr, h, d], partner, MESH
        )

    def parrive(ph, dr, d, h):
        ref = piece(ph, source(1 - dr, d), 1 - c, h)
        return pltpu.make_async_remote_copy(
            ref, ref, ps.at[ph.i, dr, h, d], pr.at[ph.i, dr, h, d], partner, MESH
        )

    def start_own(ph):
        for h in range(ph.nh):
            zcopy(ph, 0, 1, h).start()
            zcopy(ph, 1, 1, h).start()
        for h in range(ph.nh):
            pcopy(ph, 0, 0, h).start()

    def relay(ph, d):
        for h in range(ph.nh):
            zarrive(ph, 0, d, h).wait_recv()
            zcopy(ph, 0, d + 1, h).start()
            pcopy(ph, 0, d, h).start()
            zarrive(ph, 1, d, h).wait_recv()

            @pl.when(d < NB)
            def _():
                zcopy(ph, 1, d + 1, h).start()

            pcopy(ph, 1, d, h).start()

    def relay_last(ph):
        for h in range(ph.nh):
            zarrive(ph, 0, NA, h).wait_recv()
            pcopy(ph, 0, NA, h).start()

    def pwait(ph, d, both):
        for h in range(ph.nh):
            parrive(ph, 0, d, h).wait_recv()
            if both:
                parrive(ph, 1, d, h).wait_recv()

    def pwait_all(ph):
        pwait(ph, 0, False)

        @pl.loop(1, NA)
        def _(d):
            pwait(ph, d, True)

        pwait(ph, NA, False)

    def drain(ph):
        for h in range(ph.nh):
            pcopy(ph, 0, 0, h).wait_send()
            zcopy(ph, 0, NA, h).wait_send()
            pcopy(ph, 0, NA, h).wait_send()

            @pl.loop(1, NA)
            def _(d):
                zcopy(ph, 0, d, h).wait_send()
                zcopy(ph, 1, d, h).wait_send()
                pcopy(ph, 0, d, h).wait_send()
                pcopy(ph, 1, d, h).wait_send()

    def plane(src, dst, ssem, rsem, k):
        return pltpu.make_async_remote_copy(
            src, dst, ssem.at[k], rsem.at[t], (seq, rel(k)), MESH
        )

    def plane_arrive(dst, ssem, rsem, k):
        other = rel(k)
        return pltpu.make_async_remote_copy(
            dst.at[other], dst.at[other], ssem.at[k], rsem.at[other], (seq, other), MESH
        )

    def local(i, src, dst):
        return pltpu.make_async_copy(src, dst, ls.at[i])

    own = pl.ds(pl.multiple_of(c * 128, 128), 128)
    loads = [
        local(0, tok_ref, x.at[t]),
        local(1, lq_ref, w1.at[z, own, pl.ds(0, 768)]),
        local(2, fi_ref, w1.at[z, own, pl.ds(768, 128)]),
        local(3, lo_ref, w2.at[z, own, pl.ds(0, 256)]),
        local(4, fo_ref, w2.at[z, own, pl.ds(256, 128)]),
        local(5, hq_ref, w3.at[z, own]),
        local(6, ho_ref, w4.at[z, own]),
    ]
    for ld in loads:
        ld.start()

    barrier = pltpu.get_barrier_semaphore()
    far = (seq + S + 2 * c - 1) % S
    for dev in (partner, nxt[0], nxt[1], (far, t)):
        pl.semaphore_signal(barrier, inc=1, device_id=dev, device_id_type=MESH)

    @pl.loop(1, T)
    def _(k):
        pl.semaphore_signal(barrier, inc=1, device_id=(seq, rel(k)), device_id_type=MESH)

    for ld in loads:
        ld.wait()
    pl.semaphore_wait(barrier, T + 3)

    start_own(p1)

    @pl.loop(1, T)
    def _(k):
        plane(x.at[t], x.at[t], ts, tr, k).start()

    @pl.loop(1, NA)
    def _(d):
        relay(p1, d)

    start_own(p2)
    relay_last(p1)

    @pl.loop(1, T)
    def _(k):
        plane_arrive(x, ts, tr, k).wait_recv()
        plane(x.at[t], x.at[t], ts, tr, k).wait_send()

    def square(k, total):
        v = x[k].astype(F32)
        return total + jnp.sum(v * v, axis=-1, keepdims=True)

    total = lax.fori_loop(0, T, square, jnp.zeros((256, 1), F32))
    factor = lax.rsqrt(total * (1.0 / cfg.d) + 1e-06)

    @pl.loop(0, T)
    def _(k):
        x[k] = (x[k].astype(F32) * factor).astype(BF)

    def project(k0, k1):
        @pl.loop(k0, k1)
        def _(k):
            acc[...] += nn(x[k], w1[k])

    def attend(g, h):
        q = qb[h, g * 128 : (g + 1) * 128]
        s_own = nt(q, kvb[:, h * 128 : (h + 1) * 128]) * scale
        s_far = nt(q, halo[g, :, h * 128 : (h + 1) * 128]) * scale
        edge = seq == (0 if g == 0 else S - 1)
        s_far = s_far + jnp.where(edge, NEGATIVE, 0.0)
        top = jnp.maximum(
            jnp.max(s_own, axis=-1, keepdims=True), jnp.max(s_far, axis=-1, keepdims=True)
        )
        e_own = jnp.exp(s_own - top)
        e_far = jnp.exp(s_far - top)
        norm = jnp.sum(e_own, axis=-1, keepdims=True) + jnp.sum(e_far, axis=-1, keepdims=True)
        mix = nn(e_own.astype(BF), kvb[:, 256 + h * 128 : 384 + h * 128])
        mix += nn(e_far.astype(BF), halo[g, :, 256 + h * 128 : 384 + h * 128])
        act[g * 128 : (g + 1) * 128, h * 128 : (h + 1) * 128] = (mix / norm).astype(BF)

    def halo_copy(i):
        dst, dev = (halo.at[1], left) if i == 0 else (halo.at[0], right)
        return pltpu.make_async_remote_copy(
            kvb.at[pl.ds(i * 128, 128)], dst, hls.at[i], hlr.at[1 - i], dev, MESH
        )

    def halo_arrive(i):
        dev = left if i == 0 else right
        return pltpu.make_async_remote_copy(
            halo.at[i], halo.at[i], hls.at[i], hlr.at[i], dev, MESH
        )

    def finish_light():
        v = acc[...].astype(BF)
        for h in range(2):
            o = h * 384
            qb[h] = v[:, o : o + 128]
            kvb[:, h * 128 : (h + 1) * 128] = v[:, o + 128 : o + 256]
            kvb[:, 256 + h * 128 : 384 + h * 128] = v[:, o + 256 : o + 384]
        act[:, 256:384] = gelu(acc[:, 768:896]).astype(BF)
        halo_copy(0).start()
        halo_copy(1).start()

    def first():
        pwait_all(p1)
        acc[...] = jnp.zeros_like(acc)
        project(0, T // 2)

    def second():
        project(T // 2, T)

    def pick():
        @pl.loop(0, T)
        def _(k):
            picked[k] = nn(sel_ref[...], x[k]).astype(BF)

    def first_attend():
        halo_arrive(0).wait_recv()
        halo_arrive(1).wait_recv()
        attend(0, 0)

    jobs = [
        first,
        second,
        finish_light,
        pick,
        first_attend,
        lambda: attend(0, 1),
        lambda: attend(1, 0),
        lambda: attend(1, 1),
    ]
    for d in range(1, NA + 1):
        if d < NA:
            relay(p2, d)
        else:
            start_own(p3)
            relay_last(p2)
        for job in jobs[(d - 1) * 8 // NA : d * 8 // NA]:
            job()

    pwait_all(p2)
    hacc[...] = jnp.zeros_like(hacc)

    def send_out(k):
        other = rel(k)
        rs_send[k] = nt(act[...], w2[other]).astype(BF)
        plane(rs_send.at[k], rs_recv.at[t], rss, rsr, k).start()

    rs_recv[t] = nt(act[...], w2[t]).astype(BF)

    def heavy_block(zz):
        hacc[...] += nn(picked[zz], w3[zz])

    per = -(-(T - 1) // NB)

    @pl.loop(1, NA)
    def _(d):
        relay(p3, d)
        for i in range(per):
            k = (d - 1) * per + 1 + i

            @pl.when(k < T)
            def _():
                send_out(k)

        @pl.when(d > 1)
        def _():
            pwait(p3, d - 1, True)
            heavy_block(zmod(z + d - 1))
            heavy_block(zmod(z - d + 1))

    start_own(p4)
    relay_last(p3)
    pwait(p3, 0, False)
    heavy_block(z)
    pwait(p3, NB, True)
    heavy_block(zmod(z + NB))
    heavy_block(zmod(z - NB))
    pwait(p3, NA, False)
    heavy_block(zmod(z + NA))

    hv = hacc[...].astype(BF)
    mine = pl.ds(pl.multiple_of(seq * 32, 32), 32)
    for h in range(2):
        o = h * 384
        hq[h] = hv[:, o : o + 128]
        kvg[mine, h * 128 : (h + 1) * 128] = hv[:, o + 128 : o + 256]
        kvg[mine, 256 + h * 128 : 384 + h * 128] = hv[:, o + 256 : o + 384]
    kvg[mine, 512:640] = kmask_ref[...]
    start_own(pk)

    @pl.loop(1, NA)
    def _(d):
        relay(pk, d)
        relay(p4, d)

    relay_last(pk)
    relay_last(p4)

    osum[...] = rs_recv[t].astype(F32)

    @pl.loop(1, T)
    def _(k):
        plane_arrive(rs_recv, rss, rsr, k).wait_recv()
        osum[...] += rs_recv[rel(k)].astype(F32)

    pwait_all(pk)
    pwait_all(p4)
    ones = (lax.broadcasted_iota(jnp.int32, (32, 128), 1) == 0).astype(F32).astype(BF)
    bias = nt(ones, kvg[:, 512:640])
    heads = []
    for h in range(2):
        s = nt(hq[h], kvg[:, h * 128 : (h + 1) * 128]) * scale + bias
        top = jnp.max(s, axis=-1, keepdims=True)
        e = jnp.exp(s - top)
        norm = jnp.sum(e, axis=-1, keepdims=True)
        heads.append((nn(e.astype(BF), kvg[:, 256 + h * 128 : 384 + h * 128]) / norm).astype(BF))
    hh = jnp.concatenate(heads, axis=1)
    picked[0] = hh

    @pl.loop(1, T)
    def _(k):
        hs_send[k] = nt(picked[0], w4[rel(k)]).astype(BF)
        plane(hs_send.at[k], hs_recv.at[t], hss, hsr, k).start()

    hsum = nt(picked[0], w4[t]).astype(BF).astype(F32)

    def collect(k, total):
        plane_arrive(hs_recv, hss, hsr, k).wait_recv()
        return total + hs_recv[rel(k)].astype(F32)

    hsum = lax.fori_loop(1, T, collect, hsum)
    high = hsum.astype(BF)
    low = (hsum - high.astype(F32)).astype(BF)
    spread = nn(selt_ref[...], high) + nn(selt_ref[...], low)
    out_ref[...] = (osum[...] + spread).astype(BF)

    for ph in (p1, p2, p3, p4, pk):
        drain(ph)
    halo_copy(0).wait_send()
    halo_copy(1).wait_send()

    @pl.loop(1, T)
    def _(k):
        plane(rs_send.at[k], rs_recv.at[t], rss, rsr, k).wait_send()
        plane(hs_send.at[k], hs_recv.at[t], hss, hsr, k).wait_send()


def solution(mesh):
    seq_n, tp_n = mesh.shape["seq"], mesh.shape["tp"]
    side = int(round(tp_n ** 0.5))
    cfg = types.SimpleNamespace(z=seq_n // 2, tp=tp_n, sx=side, sy=tp_n // side, d=seq_n * 128)
    Z, T, NA = cfg.z, cfg.tp, cfg.z // 2

    def shards(tokens, light_qkv, heavy_qkv, ffn_in, light_out, heavy_out, ffn_out, picks):
        blocks, slots = picks.shape
        place = jnp.arange(blocks, dtype=jnp.int32)[:, None] * 128 + picks
        place = jnp.where(picks >= 0, place, -1).reshape(blocks * slots)
        where = jnp.arange(256, dtype=jnp.int32)
        sel = (place[:, None] == where[None, :]).astype(BF)
        selt = (where[:, None] == place[None, :]).astype(BF)
        first = jnp.arange(128, dtype=jnp.int32)[None, :] == 0
        kmask = jnp.where((place[:, None] < 0) & first, NEGATIVE, 0.0).astype(BF)
        anyspec = pl.BlockSpec(memory_space=pl.ANY)
        vspec = pl.BlockSpec(memory_space=pltpu.VMEM)
        dma = pltpu.SemaphoreType.DMA
        return pl.pallas_call(
            functools.partial(kernel, cfg),
            out_shape=jax.ShapeDtypeStruct((256, 256), BF),
            in_specs=[anyspec] * 7 + [vspec] * 3,
            out_specs=vspec,
            scratch_shapes=[
                pltpu.VMEM((T, 256, 256), BF),
                pltpu.VMEM((Z, 256, 896), BF),
                pltpu.VMEM((Z, 256, 384), BF),
                pltpu.VMEM((Z, 256, 768), BF),
                pltpu.VMEM((Z, 256, 256), BF),
                pltpu.VMEM((Z * 64, 640), BF),
                pltpu.VMEM((256, 896), F32),
                pltpu.VMEM((2, 256, 128), BF),
                pltpu.VMEM((256, 512), BF),
                pltpu.VMEM((2, 128, 512), BF),
                pltpu.VMEM((256, 384), BF),
                pltpu.VMEM((T, 32, 256), BF),
                pltpu.VMEM((32, 768), F32),
                pltpu.VMEM((2, 32, 128), BF),
                pltpu.VMEM((T, 256, 256), BF),
                pltpu.VMEM((T, 256, 256), BF),
                pltpu.VMEM((T, 32, 256), BF),
                pltpu.VMEM((T, 32, 256), BF),
                pltpu.VMEM((256, 256), F32),
                dma((5, 2, 2, NA + 1)),
                dma((5, 2, 2, NA + 1)),
                dma((5, 2, 2, NA + 1)),
                dma((5, 2, 2, NA + 1)),
                dma((7,)),
                dma((T,)),
                dma((T,)),
                dma((T,)),
                dma((T,)),
                dma((T,)),
                dma((T,)),
                dma((2,)),
                dma((2,)),
            ],
            compiler_params=pltpu.CompilerParams(
                collective_id=0, has_side_effects=True, vmem_limit_bytes=60 * 1024 * 1024
            ),
        )(
            tokens,
            light_qkv.reshape(128, 768),
            ffn_in,
            light_out.reshape(128, 256),
            ffn_out,
            heavy_qkv.reshape(128, 768),
            heavy_out.reshape(128, 256),
            sel,
            selt,
            kmask,
        )

    in_specs = (
        P("seq", "tp"),
        P("seq", "tp", None),
        P("seq", "tp", None),
        P("seq", "tp"),
        P("seq", "tp", None),
        P("seq", "tp", None),
        P("seq", "tp"),
        P("seq", None),
    )
    return jax.shard_map(
        shards, mesh=mesh, in_specs=in_specs, out_specs=P("seq", "tp"), check_vma=False
    )
```

```python
import functools
import types

import jax
import jax.numpy as jnp
from jax import lax
from jax.experimental import pallas as pl
from jax.experimental.pallas import tpu as pltpu
from jax.sharding import PartitionSpec as P

MESH = pl.DeviceIdType.MESH
NEGATIVE = -1e30
BF = jnp.bfloat16
F32 = jnp.float32


def nt(left, right):
    return lax.dot_general(left, right, (((1,), (1,)), ((), ())), preferred_element_type=F32)


def nn(left, right):
    return jnp.dot(left, right, preferred_element_type=F32)


def gelu(v):
    return 0.5 * v * (1.0 + jnp.tanh(0.7978845608028654 * (v + 0.044715 * (v * v * v))))


def kernel(cfg, *refs):
    (tok_ref, lq_ref, fi_ref, lo_ref, fo_ref, hq_ref, ho_ref, picks_ref, out_ref) = refs[:9]
    (x, w1, w2, pg, hw, b1, b2, w3, acc, qb, kvb, halo, act) = refs[9:22]
    (part, parts, kva, hbuf, hin, rs_send, rs_recv, osum, sel, selt) = refs[22:32]
    (zs, zr, ps, pr, ls, ts, tr, rss, rsr, hls, hlr) = refs[32:43]
    (h1s, h1r, h2s, h2r, h3s, h3r, m2s, m2r, m3s, m3r, m5s, m5r) = refs[43:]
    Z, T, SX, SY = cfg.z, cfg.tp, cfg.sx, cfg.sy
    NA, NB, HN = Z // 2, Z // 2 - 1, Z // 4
    S = 2 * Z
    seq = lax.axis_index("seq")
    t = lax.axis_index("tp")
    z = seq // 2
    c = seq % 2
    sg = 1 - 2 * c
    tx, ty = t % SX, t // SX
    scale = 128.0 ** -0.5
    mine = pl.ds(pl.multiple_of(seq * 32, 32), 32)

    def zmod(v):
        return (v + 2 * Z) % Z

    def rel(k):
        return ((ty + k // SX) % SY) * SX + (tx + k % SX) % SX

    partner = (z * 2 + 1 - c, t)
    nxt = ((zmod(z + sg) * 2 + c, t), (zmod(z - sg) * 2 + c, t))
    left = ((seq + S - 1) % S, t)
    right = ((seq + 1) % S, t)

    def phase(i, buf, rows, pieces, flat=False):
        return types.SimpleNamespace(i=i, buf=buf, rows=rows, nh=pieces, flat=flat)

    p1 = phase(0, w1, 128, 4)
    p2 = phase(1, w2, 128, 4)
    pk = phase(2, pg, 32, 1, True)

    def piece(ph, zz, cc, h):
        n = ph.rows // ph.nh
        if ph.flat:
            return ph.buf.at[pl.ds(pl.multiple_of((zz * 2 + cc) * ph.rows + h * n, n), n)]
        return ph.buf.at[zz, pl.ds(pl.multiple_of(cc * ph.rows + h * n, n), n)]

    def source(dr, d):
        return zmod(z - sg * d) if dr == 0 else zmod(z + sg * d)

    def zcopy(ph, dr, d, h):
        ref = piece(ph, source(dr, d - 1), c, h)
        return pltpu.make_async_remote_copy(
            ref, ref, zs.at[ph.i, dr, h, d], zr.at[ph.i, dr, h, d], nxt[dr], MESH
        )

    def zarrive(ph, dr, d, h):
        ref = piece(ph, source(dr, d), c, h)
        return pltpu.make_async_remote_copy(
            ref, ref, zs.at[ph.i, dr, h, d], zr.at[ph.i, dr, h, d], nxt[1 - dr], MESH
        )

    def pcopy(ph, dr, d, h):
        ref = piece(ph, source(dr, d), c, h)
        return pltpu.make_async_remote_copy(
            ref, ref, ps.at[ph.i, dr, h, d], pr.at[ph.i, dr, h, d], partner, MESH
        )

    def parrive(ph, dr, d, h):
        ref = piece(ph, source(1 - dr, d), 1 - c, h)
        return pltpu.make_async_remote_copy(
            ref, ref, ps.at[ph.i, dr, h, d], pr.at[ph.i, dr, h, d], partner, MESH
        )

    def start_own(ph):
        for h in range(ph.nh):
            zcopy(ph, 0, 1, h).start()
            zcopy(ph, 1, 1, h).start()
        for h in range(ph.nh):
            pcopy(ph, 0, 0, h).start()

    def relay(ph, d, hs=None):
        for h in range(ph.nh) if hs is None else hs:
            zarrive(ph, 0, d, h).wait_recv()
            if d < NA:
                zcopy(ph, 0, d + 1, h).start()
            pcopy(ph, 0, d, h).start()
            if d < NA:
                zarrive(ph, 1, d, h).wait_recv()
                if d < NB:
                    zcopy(ph, 1, d + 1, h).start()
                pcopy(ph, 1, d, h).start()

    def pwait(ph, d, both):
        for h in range(ph.nh):
            parrive(ph, 0, d, h).wait_recv()
            if both:
                parrive(ph, 1, d, h).wait_recv()

    def pwait_all(ph):
        pwait(ph, 0, False)

        @pl.loop(1, NA)
        def _(d):
            pwait(ph, d, True)

        pwait(ph, NA, False)

    def drain(ph):
        for h in range(ph.nh):
            pcopy(ph, 0, 0, h).wait_send()
            zcopy(ph, 0, NA, h).wait_send()
            pcopy(ph, 0, NA, h).wait_send()

            @pl.loop(1, NA)
            def _(d):
                zcopy(ph, 0, d, h).wait_send()
                zcopy(ph, 1, d, h).wait_send()
                pcopy(ph, 0, d, h).wait_send()
                pcopy(ph, 1, d, h).wait_send()

    def plane(src, dst, ssem, rsem, other):
        return pltpu.make_async_remote_copy(
            src, dst, ssem.at[other], rsem.at[t], (seq, other), MESH
        )

    def plane_arrive(dst, ssem, rsem, other):
        return pltpu.make_async_remote_copy(
            dst.at[other], dst.at[other], ssem.at[other], rsem.at[other], (seq, other), MESH
        )

    def local(i, src, dst):
        return pltpu.make_async_copy(src, dst, ls.at[i])

    own = pl.ds(pl.multiple_of(c * 128, 128), 128)
    loads = [
        local(0, tok_ref, x.at[t]),
        local(1, lq_ref, w1.at[z, own, pl.ds(0, 768)]),
        local(2, fi_ref, w1.at[z, own, pl.ds(768, 128)]),
        local(3, lo_ref, w2.at[z, own, pl.ds(0, 256)]),
        local(4, fo_ref, w2.at[z, own, pl.ds(256, 128)]),
        local(5, ho_ref, w2.at[z, own, pl.ds(384, 256)]),
        local(6, hq_ref, hw),
    ]
    for ld in loads:
        ld.start()

    def greet(dev):
        pl.semaphore_signal(barrier, inc=1, device_id=dev, device_id_type=MESH)

    barrier = pltpu.get_barrier_semaphore()
    greet(partner)
    greet(((seq + S + 2 * c - 1) % S, t))

    @pl.loop(1, T)
    def _(k):
        greet((seq, rel(k)))
        greet((z * 2 + 1 - c, rel(k)))

    @pl.loop(1, Z)
    def _(k):
        greet((zmod(z + k) * 2 + c, t))

    @pl.when(t != z)
    def _():
        greet((t * 2, z))
        greet((t * 2 + 1, z))

    loads[0].wait()
    token = lax.broadcasted_iota(jnp.int32, (128, 16), 0)
    selt[...] = jnp.zeros_like(selt)
    selt[0:128, 0:16] = (token == picks_ref[0:1, :]).astype(F32)
    selt[128:256, 16:32] = (token == picks_ref[1:2, :]).astype(F32)
    select = selt[...].T[0:32]
    live = jnp.sum(select, axis=-1, keepdims=True)
    lane = lax.broadcasted_iota(jnp.int32, (32, 128), 1)
    pg[mine, 0:256] = nn(select.astype(BF), x[t]).astype(BF)
    pg[mine, 256:384] = jnp.where(lane == 0, (1.0 - live) * NEGATIVE, 0.0).astype(BF)

    for ld in loads[1:]:
        ld.wait()
    pl.semaphore_wait(barrier, 2 * (T - 1) + Z + 1 + jnp.where(t != z, 2, 0))

    PR = 256 // T

    def remote(src, dst, ssem, rsem, dev):
        return pltpu.make_async_remote_copy(src, dst, ssem, rsem, dev, MESH)

    def hpiece(m):
        return hw.at[m % 2, pl.ds(pl.multiple_of((m // 2) * PR, PR), PR)]

    def h1(m):
        return remote(hpiece(m), b1.at[t], h1s.at[m], h1r.at[t], (seq, m))

    def h1_arrive(m):
        return remote(b1.at[m], b1.at[m], h1s.at[m], h1r.at[m], (seq, m))

    def h2(zz):
        return remote(b1.at[zz], b2.at[z], h2s.at[zz], h2r.at[z], (zz * 2 + c, t))

    def h2_arrive(zz):
        return remote(b2.at[zz], b2.at[zz], h2s.at[zz], h2r.at[zz], (zz * 2 + c, t))

    def w3_rows(cc, i):
        return w3.at[pl.ds(pl.multiple_of(cc * 128 + i * PR, PR), PR)]

    def h3(j):
        dst = w3_rows(c, t // 2)
        return remote(b2.at[j], dst, h3s.at[j], h3r.at[(t // 2) * 2 + c], (z * 2 + t % 2, j))

    def h3_arrive(i, cc):
        dst = w3_rows(cc, i)
        return remote(dst, dst, h3s.at[i], h3r.at[i * 2 + cc], (z * 2 + cc, i * 2 + c))

    start_own(pk)

    @pl.loop(1, T)
    def _(k):
        h1(rel(k)).start()

    start_own(p1)

    @pl.loop(1, T)
    def _(k):
        plane(x.at[t], x.at[t], ts, tr, rel(k)).start()

    mv = local(0, hpiece(t), b1.at[t])
    mv.start()
    mv.wait()

    def second_hop():
        @pl.loop(1, T)
        def _(k):
            h1_arrive(rel(k)).wait_recv()

        @pl.loop(1, Z)
        def _(k):
            h2(zmod(z + k)).start()

        mv = local(0, b1.at[z], b2.at[z])
        mv.start()
        mv.wait()

    def third_hop():
        @pl.loop(1, Z)
        def _(k):
            h2_arrive(zmod(z + k)).wait_recv()

        @pl.loop(1, T)
        def _(k):
            h3(rel(k)).start()

        @pl.when(t % 2 != c)
        def _():
            h3(t).start()

        @pl.when(t % 2 == c)
        def _():
            keep = local(0, b2.at[t], w3_rows(c, t // 2))
            keep.start()
            keep.wait()

    def normalize():
        @pl.loop(1, T)
        def _(k):
            plane_arrive(x, ts, tr, rel(k)).wait_recv()
            plane(x.at[t], x.at[t], ts, tr, rel(k)).wait_send()

        def square(k, total):
            v = x[k].astype(F32)
            return total + jnp.sum(v * v, axis=-1, keepdims=True)

        total = lax.fori_loop(0, T, square, jnp.zeros((256, 1), F32))
        factor = lax.rsqrt(total * (1.0 / cfg.d) + 1e-06)

        @pl.loop(0, T)
        def _(k):
            x[k] = (x[k].astype(F32) * factor).astype(BF)

    def light_block(zz):
        acc[...] += nn(x[zz], w1[zz])

    def blocks(ph, block, d):
        pwait(ph, d, 0 < d < NA)
        if d == 0 or d == NA:
            block(zmod(z + d))
        else:
            block(zmod(z + d))
            block(zmod(z - d))

    def project(first, last):
        def job():
            if first == 0:
                acc[...] = jnp.zeros_like(acc)
            for d in range(first, last):
                blocks(p1, light_block, d)

        return job

    def finish_light():
        v = acc[...].astype(BF)
        for h in range(2):
            o = h * 384
            qb[h] = v[:, o : o + 128]
            kvb[:, h * 128 : (h + 1) * 128] = v[:, o + 128 : o + 256]
            kvb[:, 256 + h * 128 : 384 + h * 128] = v[:, o + 256 : o + 384]
        act[:, 256:384] = gelu(acc[:, 768:896]).astype(BF)
        halo_copy(0).start()
        halo_copy(1).start()

    def attend(g, h):
        q = qb[h, g * 128 : (g + 1) * 128]
        s_own = nt(q, kvb[:, h * 128 : (h + 1) * 128]) * scale
        s_far = nt(q, halo[g, :, h * 128 : (h + 1) * 128]) * scale
        edge = seq == (0 if g == 0 else S - 1)
        s_far = s_far + jnp.where(edge, NEGATIVE, 0.0)
        top = jnp.maximum(
            jnp.max(s_own, axis=-1, keepdims=True), jnp.max(s_far, axis=-1, keepdims=True)
        )
        e_own = jnp.exp(s_own - top)
        e_far = jnp.exp(s_far - top)
        norm = jnp.sum(e_own, axis=-1, keepdims=True) + jnp.sum(e_far, axis=-1, keepdims=True)
        mix = nn(e_own.astype(BF), kvb[:, 256 + h * 128 : 384 + h * 128])
        mix += nn(e_far.astype(BF), halo[g, :, 256 + h * 128 : 384 + h * 128])
        act[g * 128 : (g + 1) * 128, h * 128 : (h + 1) * 128] = (mix / norm).astype(BF)

    def halo_copy(i):
        dst, dev = (halo.at[1], left) if i == 0 else (halo.at[0], right)
        return pltpu.make_async_remote_copy(
            kvb.at[pl.ds(i * 128, 128)], dst, hls.at[i], hlr.at[1 - i], dev, MESH
        )

    def halo_arrive(i):
        dev = left if i == 0 else right
        return pltpu.make_async_remote_copy(
            halo.at[i], halo.at[i], hls.at[i], hlr.at[i], dev, MESH
        )

    def attend_pair(g):
        def job():
            halo_arrive(g).wait_recv()
            attend(g, 0)
            attend(g, 1)

        return job

    def m2(g):
        return remote(part.at[g], parts.at[t], m2s.at[g], m2r.at[t], (seq, g))

    def m2_arrive(g):
        return remote(parts.at[g], parts.at[g], m2s.at[g], m2r.at[g], (seq, g))

    def slots(g):
        return pl.ds(pl.multiple_of(g * 64, 64), 64)

    def m3(g):
        return remote(kva.at[slots(t)], kva.at[slots(t)], m3s.at[g], m3r.at[t], (seq, g))

    def m3_arrive(g):
        return remote(kva.at[slots(g)], kva.at[slots(g)], m3s.at[g], m3r.at[g], (seq, g))

    def m5(cc):
        src = hbuf.at[pl.ds(cc * 32, 32)]
        return remote(src, hin.at[c], m5s.at[cc], m5r.at[c], (t * 2 + cc, z))

    def m5_arrive(cc):
        return remote(hin.at[cc], hin.at[cc], m5s.at[cc], m5r.at[cc], (t * 2 + cc, z))

    def heavy_products():
        pwait_all(pk)
        for i in range(T // 2):
            for cc in range(2):

                @pl.when((i * 2 + c != t) | (c != cc))
                def _():
                    h3_arrive(i, cc).wait_recv()

        def product(g):
            rows = pg[slots(g), 0:256]
            wide = rows.astype(F32)
            square = jnp.sum(wide * wide, axis=-1, keepdims=True)
            high = square.astype(BF)
            low = (square - high.astype(F32)).astype(BF)
            lane = lax.broadcasted_iota(jnp.int32, (64, 128), 1)
            tail = jnp.where(lane == 0, high.astype(F32), jnp.where(lane == 1, low.astype(F32), 0.0))
            return nn(rows, w3[...]).astype(BF), tail.astype(BF)

        @pl.loop(1, T)
        def _(k):
            g = rel(k)
            part[g, :, 0:384], part[g, :, 384:512] = product(g)
            m2(g).start()

        parts[t, :, 0:384], parts[t, :, 384:512] = product(t)

    def heavy_pairs():
        def gather(k, total):
            m2_arrive(rel(k)).wait_recv()
            return total + parts[rel(k)].astype(F32)

        total = lax.fori_loop(1, T, gather, parts[t].astype(F32))
        square = total[:, 384:385] + total[:, 385:386]
        v = (total[:, 0:384] * lax.rsqrt(square * (1.0 / cfg.d) + 1e-06)).astype(BF)
        hbuf[...] = v[:, 0:128]
        kva[slots(t), :] = v[:, 128:384]

        @pl.loop(1, T)
        def _(k):
            m3(rel(k)).start()

    def heavy_attend():
        @pl.loop(1, T)
        def _(k):
            m3_arrive(rel(k)).wait_recv()

        lane = lax.broadcasted_iota(jnp.int32, (64, 128), 1)
        bias = nt((lane == 0).astype(F32).astype(BF), pg[:, 256:384])
        s = nt(hbuf[...], kva[:, 0:128]) * scale + bias
        top = jnp.max(s, axis=-1, keepdims=True)
        e = jnp.exp(s - top)
        norm = jnp.sum(e, axis=-1, keepdims=True)
        hbuf[...] = (nn(e.astype(BF), kva[:, 128:256]) / norm).astype(BF)
        for cc in range(2):

            @pl.when((t != z) | (c != cc))
            def _():
                m5(cc).start()

            @pl.when((t == z) & (c == cc))
            def _():
                hin[cc] = hbuf[cc * 32 : (cc + 1) * 32]

    def heavy_rows():
        for cc in range(2):

            @pl.when((t != z) | (c != cc))
            def _():
                m5_arrive(cc).wait_recv()

            spread = selt[:, 0:32].astype(BF)
            act[:, 384 + cc * 128 : 512 + cc * 128] = nn(spread, hin[cc]).astype(BF)

    def send_out(other):
        value = nt(act[...], w2[other]).astype(BF)

        @pl.when(other != t)
        def _():
            rs_send[other] = value
            plane(rs_send.at[other], rs_recv.at[t], rss, rsr, other).start()

        @pl.when(other == t)
        def _():
            rs_recv[t] = value

    def send_some(first, last, count, lowest):
        def job():
            @pl.loop(first, last)
            def _(k):
                send_out(zmod(z + lowest + (t + k) % count))

        return job

    near = 2 * HN + 1

    def first_sums():
        pwait(p2, 0, False)
        for d in range(1, HN + 1):
            pwait(p2, d, True)
        send_some(0, near // 3, near, -HN)()

    for u in range(1, HN + 1):
        half = p1.nh // 2
        relay(pk, 2 * u - 1)
        relay(p1, u, range(half))
        if 2 * u - 1 == max(1, NA // 4 - 1):
            second_hop()
        relay(pk, 2 * u)
        relay(p1, u, range(half, p1.nh))
        if 2 * u == max(2, 3 * NA // 4):
            third_hop()

    def spread_jobs(steps, jobs):
        for i, step in enumerate(steps):
            step()
            for job in jobs[i * len(jobs) // len(steps) : (i + 1) * len(jobs) // len(steps)]:
                job()

    def both(*jobs):
        return lambda: [job() for job in jobs]

    lap = max(1, NA // 4)

    def step_one(u):
        def step():
            if u == NA - lap + 1:
                start_own(p2)
            relay(p1, u)
            if u > NA - lap:
                relay(p2, u - NA + lap)

        return step

    last = max(HN + 1, NA - 1)
    spread_jobs(
        [step_one(u) for u in range(HN + 1, NA + 1)],
        [
            both(heavy_products, normalize),
            project(0, HN + 1),
            both(heavy_pairs, project(HN + 1, last)),
            heavy_attend,
        ],
    )
    spread_jobs(
        [functools.partial(relay, p2, u) for u in range(lap + 1, NA + 1)],
        [
            both(project(last, NA + 1), finish_light),
            attend_pair(0),
            both(attend_pair(1), heavy_rows),
            first_sums,
            send_some(near // 3, 2 * near // 3, near, -HN),
            send_some(2 * near // 3, near, near, -HN),
        ],
    )
    for d in range(HN + 1, NA + 1):
        pwait(p2, d, d < NA)
    send_some(0, Z - near, Z - near, HN + 1)()

    osum[...] = rs_recv[t].astype(F32)

    @pl.loop(1, T)
    def _(k):
        plane_arrive(rs_recv, rss, rsr, rel(k)).wait_recv()
        osum[...] += rs_recv[rel(k)].astype(F32)

    out_ref[...] = osum[...].astype(BF)

    for ph in (p1, p2, pk):
        drain(ph)
    halo_copy(0).wait_send()
    halo_copy(1).wait_send()

    @pl.loop(1, T)
    def _(k):
        other = rel(k)
        plane(rs_send.at[other], rs_recv.at[t], rss, rsr, other).wait_send()
        h1(other).wait_send()
        h3(other).wait_send()
        m2(other).wait_send()
        m3(other).wait_send()

    @pl.loop(1, Z)
    def _(k):
        h2(zmod(z + k)).wait_send()

    @pl.when(t % 2 != c)
    def _():
        h3(t).wait_send()

    for cc in range(2):

        @pl.when((t != z) | (c != cc))
        def _():
            m5(cc).wait_send()


def solution(mesh):
    seq_n, tp_n = mesh.shape["seq"], mesh.shape["tp"]
    side = int(round(tp_n ** 0.5))
    cfg = types.SimpleNamespace(z=seq_n // 2, tp=tp_n, sx=side, sy=tp_n // side, d=seq_n * 128)
    Z, T, NA = cfg.z, cfg.tp, cfg.z // 2

    def shards(tokens, light_qkv, heavy_qkv, ffn_in, light_out, heavy_out, ffn_out, picks):
        anyspec = pl.BlockSpec(memory_space=pl.ANY)
        vspec = pl.BlockSpec(memory_space=pltpu.VMEM)
        dma = pltpu.SemaphoreType.DMA
        return pl.pallas_call(
            functools.partial(kernel, cfg),
            out_shape=jax.ShapeDtypeStruct((256, 256), BF),
            in_specs=[anyspec] * 7 + [vspec],
            out_specs=vspec,
            scratch_shapes=[
                pltpu.VMEM((T, 256, 256), BF),
                pltpu.VMEM((Z, 256, 896), BF),
                pltpu.VMEM((Z, 256, 640), BF),
                pltpu.VMEM((Z * 64, 384), BF),
                pltpu.VMEM((2, 128, 384), BF),
                pltpu.VMEM((T, 256 // T, 384), BF),
                pltpu.VMEM((Z, 256 // T, 384), BF),
                pltpu.VMEM((256, 384), BF),
                pltpu.VMEM((256, 896), F32),
                pltpu.VMEM((2, 256, 128), BF),
                pltpu.VMEM((256, 512), BF),
                pltpu.VMEM((2, 128, 512), BF),
                pltpu.VMEM((256, 640), BF),
                pltpu.VMEM((T, 64, 512), BF),
                pltpu.VMEM((T, 64, 512), BF),
                pltpu.VMEM((Z * 64, 256), BF),
                pltpu.VMEM((64, 128), BF),
                pltpu.VMEM((2, 32, 128), BF),
                pltpu.VMEM((T, 256, 256), BF),
                pltpu.VMEM((T, 256, 256), BF),
                pltpu.VMEM((256, 256), F32),
                pltpu.VMEM((32, 256), BF),
                pltpu.VMEM((256, 128), F32),
                dma((3, 2, 4, NA + 1)),
                dma((3, 2, 4, NA + 1)),
                dma((3, 2, 4, NA + 1)),
                dma((3, 2, 4, NA + 1)),
                dma((7,)),
            ]
            + [dma((T,))] * 4
            + [dma((2,))] * 2
            + [dma((T,))] * 10
            + [dma((2,))] * 2,
            compiler_params=pltpu.CompilerParams(
                collective_id=0, has_side_effects=True, vmem_limit_bytes=60 * 1024 * 1024
            ),
        )(
            tokens,
            light_qkv.reshape(128, 768),
            ffn_in,
            light_out.reshape(128, 256),
            ffn_out,
            jnp.transpose(heavy_qkv, (1, 0, 2)),
            heavy_out.reshape(128, 256),
            picks,
        )

    in_specs = (
        P("seq", "tp"),
        P("seq", "tp", None),
        P("seq", "tp", None),
        P("seq", "tp"),
        P("seq", "tp", None),
        P("seq", "tp", None),
        P("seq", "tp"),
        P("seq", None),
    )
    return jax.shard_map(
        shards, mesh=mesh, in_specs=in_specs, out_specs=P("seq", "tp"), check_vma=False
    )
```

```python
import functools
import types

import jax
import jax.numpy as jnp
from jax import lax
from jax.experimental import pallas as pl
from jax.experimental.pallas import tpu as pltpu
from jax.sharding import PartitionSpec as P

MESH = pl.DeviceIdType.MESH
NEGATIVE = -1e30
BF = jnp.bfloat16
F32 = jnp.float32


def nt(left, right):
    return lax.dot_general(left, right, (((1,), (1,)), ((), ())), preferred_element_type=F32)


def nn(left, right):
    return jnp.dot(left, right, preferred_element_type=F32)


def gelu(v):
    return 0.5 * v * (1.0 + jnp.tanh(0.7978845608028654 * (v + 0.044715 * (v * v * v))))


def kernel(cfg, *refs):
    (tok_ref, lq_ref, fi_ref, lo_ref, fo_ref, hq_ref, ho_ref, picks_ref, out_ref) = refs[:9]
    (x, w1, w2, pg, hw, b1, b2, w3, acc, qb, kvb, halo, act) = refs[9:22]
    (part, parts, kva, hbuf, hin, rs_send, rs_recv, osum, sel, selt) = refs[22:32]
    (zs, zr, ps, pr, ls, ts, tr, rss, rsr, hls, hlr) = refs[32:43]
    (h1s, h1r, h2s, h2r, h3s, h3r, m2s, m2r, m3s, m3r, m5s, m5r) = refs[43:]
    Z, T, SX, SY = cfg.z, cfg.tp, cfg.sx, cfg.sy
    NA, NB, HN = Z // 2, Z // 2 - 1, Z // 4
    S = 2 * Z
    seq = lax.axis_index("seq")
    t = lax.axis_index("tp")
    z = seq // 2
    c = seq % 2
    sg = 1 - 2 * c
    tx, ty = t % SX, t // SX
    scale = 128.0 ** -0.5
    mine = pl.ds(pl.multiple_of(seq * 32, 32), 32)

    def zmod(v):
        return (v + 2 * Z) % Z

    def rel(k):
        return ((ty + k // SX) % SY) * SX + (tx + k % SX) % SX

    partner = (z * 2 + 1 - c, t)
    nxt = ((zmod(z + sg) * 2 + c, t), (zmod(z - sg) * 2 + c, t))
    left = ((seq + S - 1) % S, t)
    right = ((seq + 1) % S, t)

    def phase(i, buf, rows, pieces, flat=False):
        return types.SimpleNamespace(i=i, buf=buf, rows=rows, nh=pieces, flat=flat)

    p1 = phase(0, w1, 128, 2)
    p2 = phase(1, w2, 128, 2)
    pk = phase(2, pg, 32, 1, True)

    def piece(ph, zz, cc, h):
        n = ph.rows // ph.nh
        if ph.flat:
            return ph.buf.at[pl.ds(pl.multiple_of((zz * 2 + cc) * ph.rows + h * n, n), n)]
        return ph.buf.at[zz, pl.ds(pl.multiple_of(cc * ph.rows + h * n, n), n)]

    def source(dr, d):
        return zmod(z - sg * d) if dr == 0 else zmod(z + sg * d)

    def zcopy(ph, dr, d, h):
        ref = piece(ph, source(dr, d - 1), c, h)
        return pltpu.make_async_remote_copy(
            ref, ref, zs.at[ph.i, dr, h, d], zr.at[ph.i, dr, h, d], nxt[dr], MESH
        )

    def zarrive(ph, dr, d, h):
        ref = piece(ph, source(dr, d), c, h)
        return pltpu.make_async_remote_copy(
            ref, ref, zs.at[ph.i, dr, h, d], zr.at[ph.i, dr, h, d], nxt[1 - dr], MESH
        )

    def pcopy(ph, dr, d, h):
        ref = piece(ph, source(dr, d), c, h)
        return pltpu.make_async_remote_copy(
            ref, ref, ps.at[ph.i, dr, h, d], pr.at[ph.i, dr, h, d], partner, MESH
        )

    def parrive(ph, dr, d, h):
        ref = piece(ph, source(1 - dr, d), 1 - c, h)
        return pltpu.make_async_remote_copy(
            ref, ref, ps.at[ph.i, dr, h, d], pr.at[ph.i, dr, h, d], partner, MESH
        )

    def start_own(ph):
        for h in range(ph.nh):
            zcopy(ph, 0, 1, h).start()
            zcopy(ph, 1, 1, h).start()
        for h in range(ph.nh):
            pcopy(ph, 0, 0, h).start()

    def relay(ph, d, hs=None):
        for h in range(ph.nh) if hs is None else hs:
            zarrive(ph, 0, d, h).wait_recv()
            if d < NA:
                zcopy(ph, 0, d + 1, h).start()
            pcopy(ph, 0, d, h).start()
            if d < NA:
                zarrive(ph, 1, d, h).wait_recv()
                if d < NB:
                    zcopy(ph, 1, d + 1, h).start()
                pcopy(ph, 1, d, h).start()

    def pwait(ph, d, both):
        for h in range(ph.nh):
            parrive(ph, 0, d, h).wait_recv()
            if both:
                parrive(ph, 1, d, h).wait_recv()

    def pwait_all(ph):
        pwait(ph, 0, False)

        @pl.loop(1, NA)
        def _(d):
            pwait(ph, d, True)

        pwait(ph, NA, False)

    def drain(ph):
        for h in range(ph.nh):
            pcopy(ph, 0, 0, h).wait_send()
            zcopy(ph, 0, NA, h).wait_send()
            pcopy(ph, 0, NA, h).wait_send()

            @pl.loop(1, NA)
            def _(d):
                zcopy(ph, 0, d, h).wait_send()
                zcopy(ph, 1, d, h).wait_send()
                pcopy(ph, 0, d, h).wait_send()
                pcopy(ph, 1, d, h).wait_send()

    def plane(src, dst, ssem, rsem, other):
        return pltpu.make_async_remote_copy(
            src, dst, ssem.at[other], rsem.at[t], (seq, other), MESH
        )

    def plane_arrive(dst, ssem, rsem, other):
        return pltpu.make_async_remote_copy(
            dst.at[other], dst.at[other], ssem.at[other], rsem.at[other], (seq, other), MESH
        )

    def local(i, src, dst):
        return pltpu.make_async_copy(src, dst, ls.at[i])

    own = pl.ds(pl.multiple_of(c * 128, 128), 128)
    loads = [
        local(0, tok_ref, x.at[t]),
        local(1, lq_ref, w1.at[z, own, pl.ds(0, 768)]),
        local(2, fi_ref, w1.at[z, own, pl.ds(768, 128)]),
        local(3, lo_ref, w2.at[z, own, pl.ds(0, 256)]),
        local(4, fo_ref, w2.at[z, own, pl.ds(256, 128)]),
        local(5, ho_ref, w2.at[z, own, pl.ds(384, 256)]),
        local(6, hq_ref, hw),
    ]
    for ld in loads:
        ld.start()

    def greet(dev):
        pl.semaphore_signal(barrier, inc=1, device_id=dev, device_id_type=MESH)

    barrier = pltpu.get_barrier_semaphore()
    greet(partner)
    greet(((seq + S + 2 * c - 1) % S, t))

    @pl.loop(1, T)
    def _(k):
        greet((seq, rel(k)))
        greet((z * 2 + 1 - c, rel(k)))

    @pl.loop(1, Z)
    def _(k):
        greet((zmod(z + k) * 2 + c, t))

    @pl.when(t != z)
    def _():
        greet((t * 2, z))
        greet((t * 2 + 1, z))

    loads[0].wait()
    token = lax.broadcasted_iota(jnp.int32, (128, 16), 0)
    selt[...] = jnp.zeros_like(selt)
    selt[0:128, 0:16] = (token == picks_ref[0:1, :]).astype(F32)
    selt[128:256, 16:32] = (token == picks_ref[1:2, :]).astype(F32)
    select = selt[...].T[0:32]
    live = jnp.sum(select, axis=-1, keepdims=True)
    lane = lax.broadcasted_iota(jnp.int32, (32, 128), 1)
    pg[mine, 0:256] = nn(select.astype(BF), x[t]).astype(BF)
    pg[mine, 256:384] = jnp.where(lane == 0, (1.0 - live) * NEGATIVE, 0.0).astype(BF)

    for ld in loads[1:]:
        ld.wait()
    pl.semaphore_wait(barrier, 2 * (T - 1) + Z + 1 + jnp.where(t != z, 2, 0))

    PR = 256 // T

    def remote(src, dst, ssem, rsem, dev):
        return pltpu.make_async_remote_copy(src, dst, ssem, rsem, dev, MESH)

    def hpiece(m):
        return hw.at[m % 2, pl.ds(pl.multiple_of((m // 2) * PR, PR), PR)]

    def h1(m):
        return remote(hpiece(m), b1.at[t], h1s.at[m], h1r.at[t], (seq, m))

    def h1_arrive(m):
        return remote(b1.at[m], b1.at[m], h1s.at[m], h1r.at[m], (seq, m))

    def h2(zz):
        return remote(b1.at[zz], b2.at[z], h2s.at[zz], h2r.at[z], (zz * 2 + c, t))

    def h2_arrive(zz):
        return remote(b2.at[zz], b2.at[zz], h2s.at[zz], h2r.at[zz], (zz * 2 + c, t))

    def w3_rows(cc, i):
        return w3.at[pl.ds(pl.multiple_of(cc * 128 + i * PR, PR), PR)]

    def h3(j):
        dst = w3_rows(c, t // 2)
        return remote(b2.at[j], dst, h3s.at[j], h3r.at[(t // 2) * 2 + c], (z * 2 + t % 2, j))

    def h3_arrive(i, cc):
        dst = w3_rows(cc, i)
        return remote(dst, dst, h3s.at[i], h3r.at[i * 2 + cc], (z * 2 + cc, i * 2 + c))

    start_own(pk)

    @pl.loop(1, T)
    def _(k):
        h1(rel(k)).start()

    start_own(p1)

    @pl.loop(1, T)
    def _(k):
        plane(x.at[t], x.at[t], ts, tr, rel(k)).start()

    mv = local(0, hpiece(t), b1.at[t])
    mv.start()
    mv.wait()

    def second_hop():
        @pl.loop(1, T)
        def _(k):
            h1_arrive(rel(k)).wait_recv()

        @pl.loop(1, Z)
        def _(k):
            h2(zmod(z + k)).start()

        mv = local(0, b1.at[z], b2.at[z])
        mv.start()
        mv.wait()

    def third_hop():
        @pl.loop(1, Z)
        def _(k):
            h2_arrive(zmod(z + k)).wait_recv()

        @pl.loop(1, T)
        def _(k):
            h3(rel(k)).start()

        @pl.when(t % 2 != c)
        def _():
            h3(t).start()

        @pl.when(t % 2 == c)
        def _():
            keep = local(0, b2.at[t], w3_rows(c, t // 2))
            keep.start()
            keep.wait()

    def normalize():
        @pl.loop(1, T)
        def _(k):
            plane_arrive(x, ts, tr, rel(k)).wait_recv()
            plane(x.at[t], x.at[t], ts, tr, rel(k)).wait_send()

        def square(k, total):
            v = x[k].astype(F32)
            return total + jnp.sum(v * v, axis=-1, keepdims=True)

        total = lax.fori_loop(0, T, square, jnp.zeros((256, 1), F32))
        factor = lax.rsqrt(total * (1.0 / cfg.d) + 1e-06)

        @pl.loop(0, T)
        def _(k):
            x[k] = (x[k].astype(F32) * factor).astype(BF)

    def light_block(zz):
        acc[...] += nn(x[zz], w1[zz])

    def blocks(ph, block, d):
        pwait(ph, d, 0 < d < NA)
        if d == 0 or d == NA:
            block(zmod(z + d))
        else:
            block(zmod(z + d))
            block(zmod(z - d))

    def project(first, last):
        def job():
            if first == 0:
                acc[...] = jnp.zeros_like(acc)
            for d in range(first, last):
                blocks(p1, light_block, d)

        return job

    def finish_light():
        v = acc[...].astype(BF)
        for h in range(2):
            o = h * 384
            qb[h] = v[:, o : o + 128]
            kvb[:, h * 128 : (h + 1) * 128] = v[:, o + 128 : o + 256]
            kvb[:, 256 + h * 128 : 384 + h * 128] = v[:, o + 256 : o + 384]
        act[:, 256:384] = gelu(acc[:, 768:896]).astype(BF)
        halo_copy(0).start()
        halo_copy(1).start()

    def attend(g, h):
        q = qb[h, g * 128 : (g + 1) * 128]
        s_own = nt(q, kvb[:, h * 128 : (h + 1) * 128]) * scale
        s_far = nt(q, halo[g, :, h * 128 : (h + 1) * 128]) * scale
        edge = seq == (0 if g == 0 else S - 1)
        s_far = s_far + jnp.where(edge, NEGATIVE, 0.0)
        top = jnp.maximum(
            jnp.max(s_own, axis=-1, keepdims=True), jnp.max(s_far, axis=-1, keepdims=True)
        )
        e_own = jnp.exp(s_own - top)
        e_far = jnp.exp(s_far - top)
        norm = jnp.sum(e_own, axis=-1, keepdims=True) + jnp.sum(e_far, axis=-1, keepdims=True)
        mix = nn(e_own.astype(BF), kvb[:, 256 + h * 128 : 384 + h * 128])
        mix += nn(e_far.astype(BF), halo[g, :, 256 + h * 128 : 384 + h * 128])
        act[g * 128 : (g + 1) * 128, h * 128 : (h + 1) * 128] = (mix / norm).astype(BF)

    def halo_copy(i):
        dst, dev = (halo.at[1], left) if i == 0 else (halo.at[0], right)
        return pltpu.make_async_remote_copy(
            kvb.at[pl.ds(i * 128, 128)], dst, hls.at[i], hlr.at[1 - i], dev, MESH
        )

    def halo_arrive(i):
        dev = left if i == 0 else right
        return pltpu.make_async_remote_copy(
            halo.at[i], halo.at[i], hls.at[i], hlr.at[i], dev, MESH
        )

    def attend_pair(g):
        def job():
            halo_arrive(g).wait_recv()
            attend(g, 0)
            attend(g, 1)

        return job

    def m2(g):
        return remote(part.at[g], parts.at[t], m2s.at[g], m2r.at[t], (seq, g))

    def m2_arrive(g):
        return remote(parts.at[g], parts.at[g], m2s.at[g], m2r.at[g], (seq, g))

    def slots(g):
        return pl.ds(pl.multiple_of(g * 64, 64), 64)

    def m3(g):
        return remote(kva.at[slots(t)], kva.at[slots(t)], m3s.at[g], m3r.at[t], (seq, g))

    def m3_arrive(g):
        return remote(kva.at[slots(g)], kva.at[slots(g)], m3s.at[g], m3r.at[g], (seq, g))

    def m5(cc):
        src = hbuf.at[pl.ds(cc * 32, 32)]
        return remote(src, hin.at[c], m5s.at[cc], m5r.at[c], (t * 2 + cc, z))

    def m5_arrive(cc):
        return remote(hin.at[cc], hin.at[cc], m5s.at[cc], m5r.at[cc], (t * 2 + cc, z))

    def heavy_products():
        pwait_all(pk)
        for i in range(T // 2):
            for cc in range(2):

                @pl.when((i * 2 + c != t) | (c != cc))
                def _():
                    h3_arrive(i, cc).wait_recv()

        def product(g):
            rows = pg[slots(g), 0:256]
            wide = rows.astype(F32)
            square = jnp.sum(wide * wide, axis=-1, keepdims=True)
            high = square.astype(BF)
            low = (square - high.astype(F32)).astype(BF)
            lane = lax.broadcasted_iota(jnp.int32, (64, 128), 1)
            tail = jnp.where(lane == 0, high.astype(F32), jnp.where(lane == 1, low.astype(F32), 0.0))
            return nn(rows, w3[...]).astype(BF), tail.astype(BF)

        @pl.loop(1, T)
        def _(k):
            g = rel(k)
            part[g, :, 0:384], part[g, :, 384:512] = product(g)
            m2(g).start()

        parts[t, :, 0:384], parts[t, :, 384:512] = product(t)

    def heavy_pairs():
        def gather(k, total):
            m2_arrive(rel(k)).wait_recv()
            return total + parts[rel(k)].astype(F32)

        total = lax.fori_loop(1, T, gather, parts[t].astype(F32))
        square = total[:, 384:385] + total[:, 385:386]
        v = (total[:, 0:384] * lax.rsqrt(square * (1.0 / cfg.d) + 1e-06)).astype(BF)
        hbuf[...] = v[:, 0:128]
        kva[slots(t), :] = v[:, 128:384]

        @pl.loop(1, T)
        def _(k):
            m3(rel(k)).start()

    def heavy_attend():
        @pl.loop(1, T)
        def _(k):
            m3_arrive(rel(k)).wait_recv()

        lane = lax.broadcasted_iota(jnp.int32, (64, 128), 1)
        bias = nt((lane == 0).astype(F32).astype(BF), pg[:, 256:384])
        s = nt(hbuf[...], kva[:, 0:128]) * scale + bias
        top = jnp.max(s, axis=-1, keepdims=True)
        e = jnp.exp(s - top)
        norm = jnp.sum(e, axis=-1, keepdims=True)
        hbuf[...] = (nn(e.astype(BF), kva[:, 128:256]) / norm).astype(BF)
        for cc in range(2):

            @pl.when((t != z) | (c != cc))
            def _():
                m5(cc).start()

            @pl.when((t == z) & (c == cc))
            def _():
                hin[cc] = hbuf[cc * 32 : (cc + 1) * 32]

    def heavy_rows():
        for cc in range(2):

            @pl.when((t != z) | (c != cc))
            def _():
                m5_arrive(cc).wait_recv()

            spread = selt[:, 0:32].astype(BF)
            act[:, 384 + cc * 128 : 512 + cc * 128] = nn(spread, hin[cc]).astype(BF)

    def send_out(other):
        value = nt(act[...], w2[other]).astype(BF)

        @pl.when(other != t)
        def _():
            rs_send[other] = value
            plane(rs_send.at[other], rs_recv.at[t], rss, rsr, other).start()

        @pl.when(other == t)
        def _():
            rs_recv[t] = value

    def send_some(first, last, count, lowest):
        def job():
            @pl.loop(first, last)
            def _(k):
                send_out(zmod(z + lowest + (t + k) % count))

        return job

    near = 2 * HN + 1

    def first_sums():
        pwait(p2, 0, False)
        for d in range(1, HN + 1):
            pwait(p2, d, True)
        send_some(0, near // 3, near, -HN)()

    for u in range(1, HN + 1):
        half = p1.nh // 2
        relay(pk, 2 * u - 1)
        relay(p1, u, range(half))
        if 2 * u - 1 == max(1, NA // 4 - 1):
            second_hop()
        relay(pk, 2 * u)
        relay(p1, u, range(half, p1.nh))
        if 2 * u == max(2, 3 * NA // 4):
            third_hop()

    def spread_jobs(steps, jobs):
        for i, step in enumerate(steps):
            step()
            for job in jobs[i * len(jobs) // len(steps) : (i + 1) * len(jobs) // len(steps)]:
                job()

    def both(*jobs):
        return lambda: [job() for job in jobs]

    lap = max(1, NA // 2 - 1)

    def step_one(u):
        def step():
            if u == NA - lap + 1:
                start_own(p2)
            relay(p1, u)
            if u > NA - lap:
                relay(p2, u - NA + lap)

        return step

    last = max(HN + 1, NA - 1)
    spread_jobs(
        [step_one(u) for u in range(HN + 1, NA + 1)],
        [
            both(heavy_products, normalize),
            project(0, HN + 1),
            both(heavy_pairs, project(HN + 1, last)),
            heavy_attend,
        ],
    )
    spread_jobs(
        [functools.partial(relay, p2, u) for u in range(lap + 1, NA + 1)],
        [
            both(project(last, NA + 1), finish_light),
            attend_pair(0),
            both(attend_pair(1), heavy_rows),
            first_sums,
            send_some(near // 3, 2 * near // 3, near, -HN),
            send_some(2 * near // 3, near, near, -HN),
        ],
    )
    for d in range(HN + 1, NA + 1):
        pwait(p2, d, d < NA)
    send_some(0, Z - near, Z - near, HN + 1)()

    osum[...] = rs_recv[t].astype(F32)

    @pl.loop(1, T)
    def _(k):
        plane_arrive(rs_recv, rss, rsr, rel(k)).wait_recv()
        osum[...] += rs_recv[rel(k)].astype(F32)

    out_ref[...] = osum[...].astype(BF)

    for ph in (p1, p2, pk):
        drain(ph)
    halo_copy(0).wait_send()
    halo_copy(1).wait_send()

    @pl.loop(1, T)
    def _(k):
        other = rel(k)
        plane(rs_send.at[other], rs_recv.at[t], rss, rsr, other).wait_send()
        h1(other).wait_send()
        h3(other).wait_send()
        m2(other).wait_send()
        m3(other).wait_send()

    @pl.loop(1, Z)
    def _(k):
        h2(zmod(z + k)).wait_send()

    @pl.when(t % 2 != c)
    def _():
        h3(t).wait_send()

    for cc in range(2):

        @pl.when((t != z) | (c != cc))
        def _():
            m5(cc).wait_send()


def solution(mesh):
    seq_n, tp_n = mesh.shape["seq"], mesh.shape["tp"]
    side = int(round(tp_n ** 0.5))
    cfg = types.SimpleNamespace(z=seq_n // 2, tp=tp_n, sx=side, sy=tp_n // side, d=seq_n * 128)
    Z, T, NA = cfg.z, cfg.tp, cfg.z // 2

    def shards(tokens, light_qkv, heavy_qkv, ffn_in, light_out, heavy_out, ffn_out, picks):
        anyspec = pl.BlockSpec(memory_space=pl.ANY)
        vspec = pl.BlockSpec(memory_space=pltpu.VMEM)
        dma = pltpu.SemaphoreType.DMA
        return pl.pallas_call(
            functools.partial(kernel, cfg),
            out_shape=jax.ShapeDtypeStruct((256, 256), BF),
            in_specs=[anyspec] * 7 + [vspec],
            out_specs=vspec,
            scratch_shapes=[
                pltpu.VMEM((T, 256, 256), BF),
                pltpu.VMEM((Z, 256, 896), BF),
                pltpu.VMEM((Z, 256, 640), BF),
                pltpu.VMEM((Z * 64, 384), BF),
                pltpu.VMEM((2, 128, 384), BF),
                pltpu.VMEM((T, 256 // T, 384), BF),
                pltpu.VMEM((Z, 256 // T, 384), BF),
                pltpu.VMEM((256, 384), BF),
                pltpu.VMEM((256, 896), F32),
                pltpu.VMEM((2, 256, 128), BF),
                pltpu.VMEM((256, 512), BF),
                pltpu.VMEM((2, 128, 512), BF),
                pltpu.VMEM((256, 640), BF),
                pltpu.VMEM((T, 64, 512), BF),
                pltpu.VMEM((T, 64, 512), BF),
                pltpu.VMEM((Z * 64, 256), BF),
                pltpu.VMEM((64, 128), BF),
                pltpu.VMEM((2, 32, 128), BF),
                pltpu.VMEM((T, 256, 256), BF),
                pltpu.VMEM((T, 256, 256), BF),
                pltpu.VMEM((256, 256), F32),
                pltpu.VMEM((32, 256), BF),
                pltpu.VMEM((256, 128), F32),
                dma((3, 2, 2, NA + 1)),
                dma((3, 2, 2, NA + 1)),
                dma((3, 2, 2, NA + 1)),
                dma((3, 2, 2, NA + 1)),
                dma((7,)),
            ]
            + [dma((T,))] * 4
            + [dma((2,))] * 2
            + [dma((T,))] * 10
            + [dma((2,))] * 2,
            compiler_params=pltpu.CompilerParams(
                collective_id=0, has_side_effects=True, vmem_limit_bytes=60 * 1024 * 1024
            ),
        )(
            tokens,
            light_qkv.reshape(128, 768),
            ffn_in,
            light_out.reshape(128, 256),
            ffn_out,
            jnp.transpose(heavy_qkv, (1, 0, 2)),
            heavy_out.reshape(128, 256),
            picks,
        )

    in_specs = (
        P("seq", "tp"),
        P("seq", "tp", None),
        P("seq", "tp", None),
        P("seq", "tp"),
        P("seq", "tp", None),
        P("seq", "tp", None),
        P("seq", "tp"),
        P("seq", None),
    )
    return jax.shard_map(
        shards, mesh=mesh, in_specs=in_specs, out_specs=P("seq", "tp"), check_vma=False
    )
```
